32 devices in a mesh: expert: 8 (over y, x, core), dp: 4 (over z).
Axes of the slice: x: 2, y: 2, z: 4, core: 2. Of those that a mesh axis runs over, the one named last changes fastest.
Arguments:
- out_grad: bfloat16 [512, 2048], P(('expert', 'dp')), may hold values from -2.5 to 2.5
- expert_ids: int32 [512, 8], P(('expert', 'dp')), may hold values from 0 to 15, all different within a row; in each aligned block of 16 rows (0 to 15, 16 to 31, ...) at most 16 rows name the same one
- route_weights: float32 [512, 8], P(('expert', 'dp')), may hold values from 0.1 to 1
- saved_hidden: bfloat16 [16, 512, 768], P('expert', 'dp'), may hold values from -3 to 3
- w_down: bfloat16 [16, 768, 2048], P('expert'), may hold values from -0.21875 to 0.21875
- swap_flags: int32 [8, 4], P(None, 'dp'), may hold values from 0 to 1, as said below
Outputs:
- hidden_grad: bfloat16 [16, 512, 768], P('expert', 'dp')
- down_grad: bfloat16 [16, 768, 2048], P('expert', None, 'dp')
The draws below stay inside these ranges and needn't reach their ends.
Inputs may be any that keep to these rules, and one draw needn't show every extreme that they name: `expert_ids`: among the tokens of one device (aligned blocks of 16 tokens) no expert is chosen more than 16 times, and in every draw some expert is chosen exactly 16 times by one device. swap_flags[i, g] equals swap_flags[i + h, g] with h half of 8; rows 0 and h - 1 carry 1 in every group, the other rows are independent bits.
All inputs are finite; a program needn't handle non-finite values.
Results may differ from the reference program's by a relative error of at most 0.014.
Values may be sent and summed in bfloat16 or wider, within the bound.
A program may use at most 64 MiB of HBM per device.

```python
import math
import jax
import jax.numpy as jnp
import numpy as np
from jax import lax

D = 2048
FF = 768
TOPK = 8
TOK_DEV = 16
HOSTS = 8
EXPERTS = 16
TOKENS = 512
MOST = 16
SLOTS = 512
N_EXPERT = 8
N_DP = 4


def draw_swap_flags(key, part):
    half_pairs = HOSTS // 2
    bits = jax.random.randint(key, (half_pairs, N_DP), 0, 2).astype(jnp.int32)
    row_range = jnp.arange(half_pairs, dtype=jnp.int32)[:, None]
    forced = (row_range == 0) | (row_range == half_pairs - 1)
    flags_first = jnp.where(forced, 1, bits).astype(jnp.int32)
    return jnp.concatenate([flags_first, flags_first], axis=0)


def shard_levels(rng, shape, shards, smallest, top_value):
    def one(dim, shards_of):
        heights = jax.random.uniform(jax.random.fold_in(jax.random.fold_in(rng, 6), dim), (shards_of,), jnp.float32, smallest / len(shards), top_value / len(shards))
        return jnp.repeat(jnp.exp(heights), shape[dim] // shards_of).reshape((-1,) + (1,) * (len(shape) - dim - 1))

    loudness = one(*shards[0])
    for cut in shards[1:]:
        loudness = loudness * one(*cut)
    return loudness


def assign_block(rng, own, number, rows, count, top, most, slope):
    order = jax.random.permutation(rng, count)
    heavy_load, usual = portions_of(count, rows * top, most, slope, True), portions_of(count, rows * top, most, slope, False)
    places = jnp.arange(count)

    def named(lengths, offset_by):
        used = int((lengths > 0).sum())
        fixed = max(1, used // 4)
        moved = fixed + (places - fixed + offset_by * (used - fixed)) % max(1, count - fixed)
        return jnp.zeros((count,), jnp.int32).at[order[jnp.where(places < fixed, places, moved)]].set(jnp.asarray(lengths, jnp.int32))

    lengths = jnp.where(number % 4 == 0, named(heavy_load, number // 4), named(usual, number - number // 4 - 1))
    mixed = jax.random.permutation(jax.random.fold_in(own, 3), count)
    donor, taker = mixed[0:count // 2 * 2:2], mixed[1:count // 2 * 2:2]
    margin = jnp.minimum(lengths[donor] - 1, most - lengths[taker]) // 2
    margin = jnp.where((donor == order[0]) | (taker == order[0]) | (lengths[taker] == 0), 0, jnp.maximum(margin, 0))
    moved = jax.random.randint(jax.random.fold_in(own, 4), (count // 2,), 0, 1 << 20) % (margin + 1)
    lengths = lengths.at[donor].add(-moved).at[taker].add(moved)
    items = jnp.searchsorted(jnp.cumsum(lengths), jnp.arange(rows * top), side="right").astype(jnp.int32)
    listing = items.reshape(top, rows).T
    listing = listing[jax.random.permutation(jax.random.fold_in(own, 1), rows)]
    offset_by = jax.random.randint(jax.random.fold_in(own, 2), (rows, 1), 0, top)
    return jnp.take_along_axis(listing, (jnp.arange(top)[None, :] + offset_by) % top, axis=1)


def portions_of(count, total, bound, skew, full):
    weights = [(1 << 20) // math.isqrt(grade ** skew) + 1 for grade in range(1, count + 1)]
    largest = bound if full else min(bound, max(-(-total // count), total * weights[0] // sum(weights)))
    least = 1 if total - largest >= count - 1 else 0
    holding, rest = [largest] + [least] * (count - 1), total - largest - least * (count - 1)
    while rest > 0:
        candidates = [i for i in range(1, count) if holding[i] < largest] or [i for i in range(1, count) if holding[i] < bound]
        pool, left = sum([weights[i] for i in candidates]), rest
        for i in candidates:
            addition = min(bound - holding[i], max(1, left * weights[i] // pool), rest)
            holding[i] = holding[i] + addition
            rest = rest - addition
    return np.array(holding)


def scatter_about(key, dims, spread, bound, split=(), kind=jnp.bfloat16):
    array = jax.random.normal(key, dims, jnp.float32) * spread
    if len(split) > 0:
        array = shard_levels(key, dims, split, -0.22, 0.18) * array
    return jnp.clip(array, min=-bound, max=bound).astype(kind)


def setup_inputs(seed: int = 0) -> dict:
    splits = jax.random.split(jax.random.key(seed), 7)
    out_grad = scatter_about(splits[0], (TOKENS, D), 0.25, 2.5, ((0, 32),))
    expert_ids_keys = jax.random.split(jax.random.fold_in(splits[1], 1), TOKENS // TOK_DEV)
    expert_ids_turns = jax.random.permutation(jax.random.fold_in(splits[1], 3), TOKENS // TOK_DEV)
    expert_ids = jax.vmap(lambda own, number: assign_block(jax.random.fold_in(splits[1], 2), own, number, TOK_DEV, EXPERTS, TOPK, MOST, 1))(expert_ids_keys, expert_ids_turns).reshape((TOKENS, TOPK))
    route_weights = jnp.clip(0.1 + 0.9 * jax.random.uniform(splits[2], (TOKENS, TOPK), jnp.float32) ** shard_levels(splits[2], (TOKENS, TOPK), ((0, 32),), -0.2, 0.2), 0.1, 1.0)
    saved_hidden = scatter_about(splits[3], (EXPERTS, SLOTS, FF), 0.5, 3.0, ((0, 8), (1, 4)))
    w_down = scatter_about(splits[4], (EXPERTS, FF, D), FF ** -0.5, 0.21875, ((0, 8),))
    swap_flags = draw_swap_flags(jax.random.fold_in(splits[6], 71), 0)
    return dict(out_grad=out_grad, expert_ids=expert_ids, route_weights=route_weights, saved_hidden=saved_hidden, w_down=w_down, swap_flags=swap_flags)


def reference(out_grad, expert_ids, route_weights, saved_hidden, w_down, swap_flags):
    host_slots = HOSTS * MOST
    routed = TOK_DEV * TOPK
    device_count = N_EXPERT * N_DP
    chosen = expert_ids.reshape(device_count, routed)
    expert_range = jnp.arange(EXPERTS, dtype=jnp.int32)
    one_hot = (chosen[:, :, None] == expert_range[None, None, :]).astype(jnp.int32)
    position = jnp.sum((jnp.cumsum(one_hot, axis=1) - 1) * one_hot, axis=2)
    device_index = jnp.arange(device_count, dtype=jnp.int32)[:, None]
    host_index = device_index // N_DP
    group_index = device_index % N_DP
    slot_flat = (chosen * SLOTS + group_index * host_slots + host_index * MOST + position).reshape(-1).astype(jnp.int32)
    token_index = jnp.repeat(jnp.arange(TOKENS, dtype=jnp.int32), TOPK)
    table_token = jnp.zeros((EXPERTS * SLOTS,), jnp.int32).at[slot_flat].set(token_index)
    table_weight = jnp.zeros((EXPERTS * SLOTS,), jnp.float32).at[slot_flat].set(route_weights.reshape(-1))

    def per_expert(expert):
        row_start = (expert * SLOTS).astype(jnp.int32)
        rows_token = lax.dynamic_slice_in_dim(table_token, row_start, SLOTS).astype(jnp.int32)
        rows_weight = lax.dynamic_slice_in_dim(table_weight, row_start, SLOTS)
        cotangent = (rows_weight[:, None] * out_grad[rows_token].astype(jnp.float32)).astype(jnp.bfloat16)
        down_weight = w_down[expert]
        hidden_grad = jnp.dot(cotangent, down_weight.T, preferred_element_type=jnp.float32).astype(jnp.bfloat16)
        hidden_rows = saved_hidden[expert].astype(jnp.float32).reshape(N_DP, host_slots, FF)
        grad_rows = cotangent.astype(jnp.float32).reshape(N_DP, host_slots, D)
        product = jnp.einsum("grf,grd->gfd", hidden_rows, grad_rows)
        narrow = lax.optimization_barrier(product.astype(jnp.bfloat16))
        expert_grad = jnp.sum(narrow.astype(jnp.float32), axis=0).astype(jnp.bfloat16)
        return hidden_grad, expert_grad

    results = lax.map(per_expert, expert_range)
    owner_host = expert_range // 2
    flag_table = swap_flags[owner_host]
    relocated = (expert_range[:, None] % 2 == 1) & (flag_table == 1)
    partner = (((owner_host + HOSTS // 2) % HOSTS) * 2 + 1)[:, None]
    resident = jnp.where(relocated, partner, expert_range[:, None]).astype(jnp.int32)
    grads = results[1].reshape(EXPERTS, FF, N_DP, D // N_DP)
    group_range = jnp.arange(N_DP, dtype=jnp.int32)
    picked = grads[resident, :, group_range[None, :], :]
    down_grad = jnp.transpose(picked, (0, 2, 1, 3)).reshape(EXPERTS, FF, D)
    return results[0], down_grad
```

```python
import functools

import jax
import jax.numpy as jnp
from jax import lax
from jax.experimental import pallas as pl
from jax.experimental.pallas import tpu as pltpu
from jax.sharding import PartitionSpec as P

MESH = pl.DeviceIdType.MESH
LANES = 128


def dot(a, b, dims):
    return lax.dot_general(a, b, (dims, ((), ())), preferred_element_type=jnp.float32)


def kernel(
    hosts, groups, capacity,
    grad_ref, ids_ref, weight_ref, flags_ref, hidden_hbm, down_hbm,
    hidden_out, down_out,
    hid, mate, wts, full, cols, table, gbuf, total, down,
    local_sem,
    zs_sem, zr_sem,
    ps_sem, pr_sem,
    ss_sem, sr_sem,
    hs_sem, hr_sem,
    ys_sem, yr_sem,
):
    half = hosts // 2
    me = lax.axis_index("expert")
    g = lax.axis_index("dp")
    core, place = lax.rem(me, 2), lax.div(me, 2)
    sibling = me + 1 - 2 * core
    partner = lax.rem(me + half, hosts)
    tokens, width = grad_ref.shape
    slots, units = hidden_hbm.shape[1:]
    share = width // groups
    count = hosts * tokens

    def to(host, group):
        return {"expert": host, "dp": group}

    def remote(src, dst, send, recv, host, group):
        return pltpu.make_async_remote_copy(
            src_ref=src, dst_ref=dst, send_sem=send, recv_sem=recv,
            device_id=(host, group), device_id_type=MESH,
        )

    def share_of(group):
        return pl.ds(pl.multiple_of(group * share, LANES), share)

    lane = lax.broadcasted_iota(jnp.int32, (tokens, LANES), 1)
    dense = jnp.zeros((tokens, LANES), jnp.float32)
    for k in range(ids_ref.shape[1]):
        dense = dense + jnp.where(ids_ref[:, k : k + 1] == lane, weight_ref[:, k : k + 1], 0.0)
    wts[g, core, place] = dense

    own = [
        pltpu.make_async_copy(grad_ref.at[:, share_of(g)], cols.at[g, core, place], local_sem.at[0]),
        pltpu.make_async_copy(grad_ref, full.at[core, place], local_sem.at[1]),
        pltpu.make_async_copy(hidden_hbm, hid.at[g], local_sem.at[2]),
        pltpu.make_async_copy(down_hbm, down, local_sem.at[3]),
    ]
    for copy in own:
        copy.start()

    barrier = pltpu.get_barrier_semaphore()

    @pl.loop(1, groups)
    def _(d):
        pl.semaphore_signal(barrier, inc=1, device_id=(me, lax.rem(g + d, groups)), device_id_type=MESH)

    @pl.loop(1, half)
    def _(d):
        pl.semaphore_signal(barrier, inc=1, device_id=(lax.rem(me + 2 * d, hosts), g), device_id_type=MESH)

    pl.semaphore_signal(barrier, inc=1, device_id=(sibling, g), device_id_type=MESH)
    pl.semaphore_wait(barrier, groups + half - 1)

    def z_copies(d, sender):
        q = lax.rem(g + groups - d, groups) if sender else lax.rem(g + d, groups)
        slot = q if sender else g
        return (
            remote(grad_ref.at[:, share_of(q)], cols.at[slot, core, place], zs_sem.at[d, 0], zr_sem.at[d, 0], me, q),
            remote(wts.at[g, core, place], wts.at[slot, core, place], zs_sem.at[d, 1], zr_sem.at[d, 1], me, q),
        )

    @pl.loop(1, groups)
    def _(d):
        for copy in z_copies(d, False):
            copy.start()

    def p_copy(d, kind, peer_place):
        peer = lax.rem(me + 2 * d, hosts)
        src, dst = (
            (grad_ref, full.at[core, peer_place]),
            (cols.at[:, core, peer_place], cols.at[:, core, peer_place]),
            (wts.at[:, core, peer_place], wts.at[:, core, peer_place]),
        )[kind]
        return remote(src, dst, ps_sem.at[d, kind], pr_sem.at[d, kind], peer, g)

    @pl.loop(1, half)
    def _(d):
        p_copy(d, 0, place).start()

    def h_copy(way, block, expert):
        target = g + 1 if way == 0 else g - 1
        part = hid.at[block, expert]
        return remote(part, part, hs_sem.at[way, block, expert], hr_sem.at[block, expert], me, target)

    def y_copy(block):
        return remote(hid.at[block, 1], mate.at[block], ys_sem.at[block], yr_sem.at[block], partner, g)

    own[2].wait()

    def forward(block, expert):
        @pl.when((g < groups - 1) & (block <= g))
        def _():
            h_copy(0, block, expert).start()

        @pl.when((g > 0) & (block >= g))
        def _():
            h_copy(1, block, expert).start()

    forward(g, 1)
    forward(g, 0)

    own[0].wait()
    own[1].wait()

    @pl.loop(1, groups)
    def _(d):
        for copy in z_copies(d, True):
            copy.wait_recv()

    @pl.loop(1, half)
    def _(d):
        p_copy(d, 1, place).start()
        p_copy(d, 2, place).start()

    y_copy(g).start()

    @pl.loop(1, half)
    def _(d):
        source = lax.rem(place + half - d, half)
        for kind in range(3):
            p_copy(d, kind, source).wait_recv()

    def s_copy(kind, c):
        src = (full.at[c], cols.at[:, c], wts.at[:, c])[kind]
        return remote(src, src, ss_sem.at[kind], sr_sem.at[kind], sibling, g)

    for kind in range(3):
        s_copy(kind, core).start()

    def arrive(block, expert):
        @pl.when((block >= 0) & (block < groups))
        def _():
            h_copy(0, block, expert).wait_recv()
            forward(block, expert)
            if expert == 1:
                y_copy(block).start()

    for block in (g - 1, g + 1):
        arrive(block, 1)

    for kind in range(3):
        s_copy(kind, 1 - core).wait_recv()

    flag = flags_ref[pl.ds(me, 1), :].astype(jnp.float32)
    shift = tokens.bit_length() - 1
    early = lax.broadcasted_iota(jnp.int32, (count, count), 0)
    late = lax.broadcasted_iota(jnp.int32, (count, count), 1)
    before = (early < late) & (lax.shift_right_logical(early, shift) == lax.shift_right_logical(late, shift))
    before = jnp.where(before, 1.0, 0.0).astype(jnp.bfloat16)
    block_of = lax.shift_right_logical(lax.broadcasted_iota(jnp.int32, (1, count), 1), shift)
    host_of = jnp.where(block_of >= half, 2 * (block_of - half) + 1, 2 * block_of)
    slot_iota = lax.broadcasted_iota(jnp.int32, (slots, count), 0)

    def selection(q, which):
        expert = 2 * (partner if which == 2 else me) + (0 if which == 0 else 1)
        weight = table[0, pl.ds(expert, 1), :]
        position = table[1, pl.ds(expert, 1), :].astype(jnp.int32)
        slot = jnp.where(weight > 0.0, host_of * capacity + position, -1)
        hit = slot_iota == slot
        pick = jnp.where(hit, 1.0, 0.0)
        held = jnp.sum(jnp.where(hit, weight, 0.0), axis=1, keepdims=True)
        return pick.astype(jnp.bfloat16), held

    def fill_table(q):
        dense = wts[q].reshape(count, LANES).T
        table[0] = dense
        chosen = jnp.where(dense > 0.0, 1.0, 0.0).astype(jnp.bfloat16)
        table[1] = dot(chosen, before, ((1,), (0,)))

    @pl.loop(0, groups)
    def _(q):
        fill_table(q)
        rows = cols[q].reshape(count, share)
        for which in range(3):
            pick, held = selection(q, which)
            scale = held if which == 0 else held * (flag if which == 2 else 1.0 - flag)
            gbuf[q, which] = (dot(pick, rows, ((1,), (0,))) * scale).astype(jnp.bfloat16)

    own[3].wait()
    fill_table(g)
    everything = full[...].reshape(count, width)
    for which in range(2):
        pick, held = selection(g, which)
        slot_rows = (dot(pick, everything, ((1,), (0,))) * held).astype(jnp.bfloat16)
        hidden_out[which] = dot(slot_rows, down[which], ((1,), (1,))).astype(hidden_out.dtype)

    for block in (g - 1, g + 1):
        arrive(block, 0)

    def first(block):
        total[0] += dot(hid[block, 0], gbuf[block, 0], ((0,), (0,)))

    def second(block):
        y_copy(block).wait_recv()
        total[1] += dot(hid[block, 1], gbuf[block, 1], ((0,), (0,)))
        total[1] += dot(mate[block], gbuf[block, 2], ((0,), (0,)))

    total[...] = jnp.zeros_like(total)
    first(g)
    second(g)

    def there(block, act):
        @pl.when((block >= 0) & (block < groups))
        def _():
            act(block)

    @pl.loop(1, groups)
    def _(k):
        @pl.when(k > 1)
        def _():
            for block in (g - k, g + k):
                arrive(block, 1)

        there(g - k + 1, lambda block: pl.when(k > 1)(functools.partial(second, block)))
        there(g + k - 1, lambda block: pl.when(k > 1)(functools.partial(second, block)))

        @pl.when(k > 1)
        def _():
            for block in (g - k, g + k):
                arrive(block, 0)

        there(g - k, first)
        there(g + k, first)

    there(g - groups + 1, second)
    there(g + groups - 1, second)
    down_out[...] = total[...].astype(down_out.dtype)

    @pl.loop(1, groups)
    def _(d):
        for copy in z_copies(d, False):
            copy.wait_send()

    @pl.loop(1, half)
    def _(d):
        for kind in range(3):
            p_copy(d, kind, place).wait_send()

    for kind in range(3):
        s_copy(kind, core).wait_send()

    @pl.loop(0, groups)
    def _(block):
        y_copy(block).wait_send()
        for expert in range(2):
            @pl.when((g < groups - 1) & (block <= g))
            def _():
                h_copy(0, block, expert).wait_send()

            @pl.when((g > 0) & (block >= g))
            def _():
                h_copy(1, block, expert).wait_send()


def body(out_grad, expert_ids, route_weights, saved_hidden, w_down, swap_flags):
    hosts, groups = lax.axis_size("expert"), lax.axis_size("dp")
    local, slots, units = saved_hidden.shape
    tokens, width = out_grad.shape
    share = width // groups
    half = hosts // 2
    vmem = pl.BlockSpec(memory_space=pltpu.VMEM)
    hbm = pl.BlockSpec(memory_space=pl.ANY)
    dma = pltpu.SemaphoreType.DMA
    return pl.pallas_call(
        functools.partial(kernel, hosts, groups, slots // hosts),
        out_shape=(
            jax.ShapeDtypeStruct((local, slots, units), jnp.bfloat16),
            jax.ShapeDtypeStruct((local, units, share), jnp.bfloat16),
        ),
        in_specs=[vmem, vmem, vmem, vmem, hbm, hbm],
        out_specs=(vmem, vmem),
        scratch_shapes=[
            pltpu.VMEM((groups, local, slots, units), jnp.bfloat16),
            pltpu.VMEM((groups, slots, units), jnp.bfloat16),
            pltpu.VMEM((groups, 2, half, tokens, LANES), jnp.float32),
            pltpu.VMEM((2, half, tokens, width), jnp.bfloat16),
            pltpu.VMEM((groups, 2, half, tokens, share), jnp.bfloat16),
            pltpu.VMEM((2, LANES, hosts * tokens), jnp.float32),
            pltpu.VMEM((groups, 3, slots, share), jnp.bfloat16),
            pltpu.VMEM((local, units, share), jnp.float32),
            pltpu.VMEM(w_down.shape, jnp.bfloat16),
            dma((4,)),
            dma((groups, 2)), dma((groups, 2)),
            dma((half, 3)), dma((half, 3)),
            dma((3,)), dma((3,)),
            dma((2, groups, 2)), dma((groups, 2)),
            dma((groups,)), dma((groups,)),
        ],
        compiler_params=pltpu.CompilerParams(
            collective_id=0, has_side_effects=True, vmem_limit_bytes=60 * 1024 * 1024
        ),
    )(out_grad, expert_ids, route_weights, swap_flags, saved_hidden, w_down)


def solution(mesh):
    in_specs = (
        P(("expert", "dp"), None),
        P(("expert", "dp"), None),
        P(("expert", "dp"), None),
        P("expert", "dp", None),
        P("expert", None, None),
        P(None, "dp"),
    )
    out_specs = (P("expert", "dp", None), P("expert", None, "dp"))
    return jax.shard_map(body, mesh=mesh, in_specs=in_specs, out_specs=out_specs, check_vma=False)
```

```python
import functools

import jax
import jax.numpy as jnp
from jax import lax
from jax.experimental import pallas as pl
from jax.experimental.pallas import tpu as pltpu
from jax.sharding import PartitionSpec as P

MESH = pl.DeviceIdType.MESH
LANES = 128
VMEM_BYTES = 67_043_328
SPARE = 1024 * 1024


def dot(a, b, dims):
    return lax.dot_general(a, b, (dims, ((), ())), preferred_element_type=jnp.float32)


def kernel(
    hosts, groups, capacity,
    grad_hbm, ids_hbm, weight_hbm, flags_hbm, hidden_hbm, down_hbm,
    hidden_out, down_out,
    grad_ref, ids_ref, weight_ref, flags_ref,
    hid, mate, wts, full, cols, table, gbuf, total, down,
    local_sem,
    zs_sem, zr_sem,
    ps_sem, pr_sem,
    ss_sem, sr_sem,
    hs_sem, hr_sem,
    ys_sem, yr_sem,
):
    half = hosts // 2
    me = lax.axis_index("expert")
    g = lax.axis_index("dp")
    core, place = lax.rem(me, 2), lax.div(me, 2)
    sibling = me + 1 - 2 * core
    partner = lax.rem(me + half, hosts)
    tokens, width = grad_ref.shape
    slots, units = hidden_hbm.shape[1:]
    share = width // groups
    count = hosts * tokens

    def to(host, group):
        return {"expert": host, "dp": group}

    def remote(src, dst, send, recv, host, group):
        return pltpu.make_async_remote_copy(
            src_ref=src, dst_ref=dst, send_sem=send, recv_sem=recv,
            device_id=(host, group), device_id_type=MESH,
        )

    def share_of(group):
        return pl.ds(pl.multiple_of(group * share, LANES), share)

    small = [
        pltpu.make_async_copy(ids_hbm, ids_ref, local_sem.at[4]),
        pltpu.make_async_copy(weight_hbm, weight_ref, local_sem.at[5]),
        pltpu.make_async_copy(grad_hbm, grad_ref, local_sem.at[6]),
        pltpu.make_async_copy(flags_hbm, flags_ref, local_sem.at[7]),
    ]
    own = [
        pltpu.make_async_copy(grad_hbm.at[:, share_of(g)], cols.at[g, core, place], local_sem.at[0]),
        pltpu.make_async_copy(grad_hbm, full.at[core, place], local_sem.at[1]),
        pltpu.make_async_copy(hidden_hbm, hid.at[g], local_sem.at[2]),
        pltpu.make_async_copy(down_hbm, down, local_sem.at[3]),
    ]
    for copy in small + own:
        copy.start()

    barrier = pltpu.get_barrier_semaphore()

    @pl.loop(1, groups)
    def _(d):
        pl.semaphore_signal(barrier, inc=1, device_id=(me, lax.rem(g + d, groups)), device_id_type=MESH)

    @pl.loop(1, half)
    def _(d):
        pl.semaphore_signal(barrier, inc=1, device_id=(lax.rem(me + 2 * d, hosts), g), device_id_type=MESH)

    pl.semaphore_signal(barrier, inc=1, device_id=(sibling, g), device_id_type=MESH)
    for copy in small:
        copy.wait()

    row = lax.broadcasted_iota(jnp.int32, (LANES, tokens), 0)
    dense = jnp.zeros((LANES, tokens), jnp.float32)
    for k in range(ids_ref.shape[0]):
        dense = dense + jnp.where(ids_ref[k : k + 1, :] == row, weight_ref[k : k + 1, :], 0.0)
    wts[g, core, place] = dense.T

    pl.semaphore_wait(barrier, groups + half - 1)

    def z_copies(d, sender):
        q = lax.rem(g + groups - d, groups) if sender else lax.rem(g + d, groups)
        slot = q if sender else g
        return (
            remote(grad_ref.at[:, share_of(q)], cols.at[slot, core, place], zs_sem.at[d, 0], zr_sem.at[d, 0], me, q),
            remote(wts.at[g, core, place], wts.at[slot, core, place], zs_sem.at[d, 1], zr_sem.at[d, 1], me, q),
        )

    @pl.loop(1, groups)
    def _(d):
        for copy in z_copies(d, False):
            copy.start()

    def p_copy(d, kind, peer_place):
        peer = lax.rem(me + 2 * d, hosts)
        src, dst = (
            (grad_ref, full.at[core, peer_place]),
            (cols.at[:, core, peer_place], cols.at[:, core, peer_place]),
            (wts.at[:, core, peer_place], wts.at[:, core, peer_place]),
        )[kind]
        return remote(src, dst, ps_sem.at[d, kind], pr_sem.at[d, kind], peer, g)

    @pl.loop(1, half)
    def _(d):
        p_copy(d, 0, place).start()

    def h_copy(way, block, expert):
        target = g + 1 if way == 0 else g - 1
        part = hid.at[block, expert]
        return remote(part, part, hs_sem.at[way, block, expert], hr_sem.at[block, expert], me, target)

    def y_copy(block):
        return remote(hid.at[block, 1], mate.at[block], ys_sem.at[block], yr_sem.at[block], partner, g)

    own[2].wait()

    def forward(block, expert):
        @pl.when((g < groups - 1) & (block <= g))
        def _():
            h_copy(0, block, expert).start()

        @pl.when((g > 0) & (block >= g))
        def _():
            h_copy(1, block, expert).start()

    forward(g, 1)
    forward(g, 0)

    own[0].wait()
    own[1].wait()

    @pl.loop(1, groups)
    def _(d):
        for copy in z_copies(d, True):
            copy.wait_recv()

    @pl.loop(1, half)
    def _(d):
        p_copy(d, 1, place).start()
        p_copy(d, 2, place).start()

    y_copy(g).start()

    @pl.loop(1, half)
    def _(d):
        source = lax.rem(place + half - d, half)
        for kind in range(3):
            p_copy(d, kind, source).wait_recv()

    def s_copy(kind, c):
        src = (full.at[c], cols.at[:, c], wts.at[:, c])[kind]
        return remote(src, src, ss_sem.at[kind], sr_sem.at[kind], sibling, g)

    for kind in range(3):
        s_copy(kind, core).start()

    def arrive(block, expert):
        @pl.when((block >= 0) & (block < groups))
        def _():
            h_copy(0, block, expert).wait_recv()
            forward(block, expert)
            if expert == 1:
                y_copy(block).start()

    for block in (g - 1, g + 1):
        arrive(block, 1)

    for kind in range(3):
        s_copy(kind, 1 - core).wait_recv()

    lane = lax.broadcasted_iota(jnp.int32, (1, hosts), 1)
    flag = jnp.sum(jnp.where(lane == me, flags_ref[...].astype(jnp.float32), 0.0), axis=1, keepdims=True)
    shift = tokens.bit_length() - 1
    early = lax.broadcasted_iota(jnp.int32, (count, count), 0)
    late = lax.broadcasted_iota(jnp.int32, (count, count), 1)
    before = (early < late) & (lax.shift_right_logical(early, shift) == lax.shift_right_logical(late, shift))
    before = jnp.where(before, 1.0, 0.0).astype(jnp.bfloat16)
    block_of = lax.shift_right_logical(lax.broadcasted_iota(jnp.int32, (1, count), 1), shift)
    host_of = jnp.where(block_of >= half, 2 * (block_of - half) + 1, 2 * block_of)
    slot_iota = lax.broadcasted_iota(jnp.int32, (slots, count), 0)

    def selection(q, which):
        expert = 2 * (partner if which == 2 else me) + (0 if which == 0 else 1)
        weight = table[0, pl.ds(expert, 1), :]
        position = table[1, pl.ds(expert, 1), :].astype(jnp.int32)
        slot = jnp.where(weight > 0.0, host_of * capacity + position, -1)
        hit = slot_iota == slot
        pick = jnp.where(hit, 1.0, 0.0)
        held = jnp.sum(jnp.where(hit, weight, 0.0), axis=1, keepdims=True)
        return pick.astype(jnp.bfloat16), held

    def fill_table(q):
        dense = wts[q].reshape(count, LANES).T
        table[0] = dense
        chosen = jnp.where(dense > 0.0, 1.0, 0.0).astype(jnp.bfloat16)
        table[1] = dot(chosen, before, ((1,), (0,)))

    @pl.loop(0, groups)
    def _(q):
        fill_table(q)
        rows = cols[q].reshape(count, share)
        for which in range(3):
            pick, held = selection(q, which)
            scale = held if which == 0 else held * (flag if which == 2 else 1.0 - flag)
            gbuf[q, which] = (dot(pick, rows, ((1,), (0,))) * scale).astype(jnp.bfloat16)

    own[3].wait()
    fill_table(g)
    everything = full[...].reshape(count, width)
    for which in range(2):
        pick, held = selection(g, which)
        slot_rows = (dot(pick, everything, ((1,), (0,))) * held).astype(jnp.bfloat16)
        hidden_out[which] = dot(slot_rows, down[which], ((1,), (1,))).astype(hidden_out.dtype)

    for block in (g - 1, g + 1):
        arrive(block, 0)

    def first(block):
        total[0] += dot(hid[block, 0], gbuf[block, 0], ((0,), (0,)))

    def second(block):
        y_copy(block).wait_recv()
        total[1] += dot(hid[block, 1], gbuf[block, 1], ((0,), (0,)))
        total[1] += dot(mate[block], gbuf[block, 2], ((0,), (0,)))

    total[...] = jnp.zeros_like(total)
    first(g)
    second(g)

    def there(block, act):
        @pl.when((block >= 0) & (block < groups))
        def _():
            act(block)

    @pl.loop(1, groups)
    def _(k):
        @pl.when(k > 1)
        def _():
            for block in (g - k, g + k):
                arrive(block, 1)

        there(g - k + 1, lambda block: pl.when(k > 1)(functools.partial(second, block)))
        there(g + k - 1, lambda block: pl.when(k > 1)(functools.partial(second, block)))

        @pl.when(k > 1)
        def _():
            for block in (g - k, g + k):
                arrive(block, 0)

        there(g - k, first)
        there(g + k, first)

    there(g - groups + 1, second)
    there(g + groups - 1, second)
    down_out[...] = total[...].astype(down_out.dtype)

    @pl.loop(1, groups)
    def _(d):
        for copy in z_copies(d, False):
            copy.wait_send()

    @pl.loop(1, half)
    def _(d):
        for kind in range(3):
            p_copy(d, kind, place).wait_send()

    for kind in range(3):
        s_copy(kind, core).wait_send()

    @pl.loop(0, groups)
    def _(block):
        y_copy(block).wait_send()
        for expert in range(2):
            @pl.when((g < groups - 1) & (block <= g))
            def _():
                h_copy(0, block, expert).wait_send()

            @pl.when((g > 0) & (block >= g))
            def _():
                h_copy(1, block, expert).wait_send()


def finish(hidden_in, down_in, hidden_out, down_out, sem):
    copies = [
        pltpu.make_async_copy(hidden_in, hidden_out, sem.at[0]),
        pltpu.make_async_copy(down_in, down_out, sem.at[1]),
    ]
    for copy in copies:
        copy.start()
    for copy in copies:
        copy.wait()


def body(out_grad, expert_ids, route_weights, saved_hidden, w_down, swap_flags):
    hosts, groups = lax.axis_size("expert"), lax.axis_size("dp")
    local, slots, units = saved_hidden.shape
    tokens, width = out_grad.shape
    share = width // groups
    half = hosts // 2
    vmem = pl.BlockSpec(memory_space=pltpu.VMEM)
    hbm = pl.BlockSpec(memory_space=pl.ANY)
    dma = pltpu.SemaphoreType.DMA
    shapes = (
        jax.ShapeDtypeStruct((local, slots, units), jnp.bfloat16),
        jax.ShapeDtypeStruct((local, units, share), jnp.bfloat16),
    )
    kept = 2 * local * units * (slots + share) + SPARE
    results = pl.pallas_call(
        functools.partial(kernel, hosts, groups, slots // hosts),
        out_shape=tuple(pltpu.VMEM(x.shape, x.dtype) for x in shapes),
        in_specs=[pl.BlockSpec(memory_space=pltpu.HBM)] * 6,
        out_specs=(vmem, vmem),
        scratch_shapes=[
            pltpu.VMEM(out_grad.shape, out_grad.dtype),
            pltpu.VMEM(expert_ids.shape[::-1], expert_ids.dtype),
            pltpu.VMEM(route_weights.shape[::-1], route_weights.dtype),
            pltpu.VMEM(swap_flags.shape[::-1], swap_flags.dtype),
            pltpu.VMEM((groups, local, slots, units), jnp.bfloat16),
            pltpu.VMEM((groups, slots, units), jnp.bfloat16),
            pltpu.VMEM((groups, 2, half, tokens, LANES), jnp.float32),
            pltpu.VMEM((2, half, tokens, width), jnp.bfloat16),
            pltpu.VMEM((groups, 2, half, tokens, share), jnp.bfloat16),
            pltpu.VMEM((2, LANES, hosts * tokens), jnp.float32),
            pltpu.VMEM((groups, 3, slots, share), jnp.bfloat16),
            pltpu.VMEM((local, units, share), jnp.float32),
            pltpu.VMEM(w_down.shape, jnp.bfloat16),
            dma((8,)),
            dma((groups, 2)), dma((groups, 2)),
            dma((half, 3)), dma((half, 3)),
            dma((3,)), dma((3,)),
            dma((2, groups, 2)), dma((groups, 2)),
            dma((groups,)), dma((groups,)),
        ],
        compiler_params=pltpu.CompilerParams(
            collective_id=0, has_side_effects=True, vmem_limit_bytes=VMEM_BYTES - kept
        ),
    )(out_grad, expert_ids.T, route_weights.T, swap_flags.T, saved_hidden, w_down)
    return pl.pallas_call(
        finish,
        out_shape=shapes,
        in_specs=[vmem, vmem],
        out_specs=(hbm, hbm),
        scratch_shapes=[dma((2,))],
        compiler_params=pltpu.CompilerParams(vmem_limit_bytes=8 * 1024 * 1024),
    )(*results)


def solution(mesh):
    in_specs = (
        P(("expert", "dp"), None),
        P(("expert", "dp"), None),
        P(("expert", "dp"), None),
        P("expert", "dp", None),
        P("expert", None, None),
        P(None, "dp"),
    )
    out_specs = (P("expert", "dp", None), P("expert", None, "dp"))
    return jax.shard_map(body, mesh=mesh, in_specs=in_specs, out_specs=out_specs, check_vma=False)
```

```python
import functools

import jax
import jax.numpy as jnp
from jax import lax
from jax.experimental import pallas as pl
from jax.experimental.pallas import tpu as pltpu
from jax.sharding import PartitionSpec as P

MESH = pl.DeviceIdType.MESH
LANES = 128
VMEM_BYTES = 67_043_328
SPARE = 1024 * 1024


def dot(a, b, dims):
    return lax.dot_general(a, b, (dims, ((), ())), preferred_element_type=jnp.float32)


def kernel(
    hosts, groups, capacity,
    grad_hbm, ids_hbm, weight_hbm, flags_hbm, hidden_hbm, down_hbm,
    hidden_out, down_out,
    grad_ref, ids_ref, weight_ref, flags_ref,
    hid, mate, wts, full, cols, table, gbuf, total, down,
    local_sem,
    zs_sem, zr_sem,
    ps_sem, pr_sem,
    ss_sem, sr_sem,
    hs_sem, hr_sem,
    ys_sem, yr_sem,
):
    half = hosts // 2
    me = lax.axis_index("expert")
    g = lax.axis_index("dp")
    core, place = lax.rem(me, 2), lax.div(me, 2)
    sibling = me + 1 - 2 * core
    partner = lax.rem(me + half, hosts)
    tokens, width = grad_ref.shape
    slots, units = hidden_hbm.shape[1:]
    share = width // groups
    count = hosts * tokens

    def to(host, group):
        return {"expert": host, "dp": group}

    def remote(src, dst, send, recv, host, group):
        return pltpu.make_async_remote_copy(
            src_ref=src, dst_ref=dst, send_sem=send, recv_sem=recv,
            device_id=(host, group), device_id_type=MESH,
        )

    def share_of(group):
        return pl.ds(pl.multiple_of(group * share, LANES), share)

    small = [
        pltpu.make_async_copy(ids_hbm, ids_ref, local_sem.at[4]),
        pltpu.make_async_copy(weight_hbm, weight_ref, local_sem.at[5]),
        pltpu.make_async_copy(grad_hbm, grad_ref, local_sem.at[6]),
        pltpu.make_async_copy(flags_hbm, flags_ref, local_sem.at[7]),
    ]
    own = [
        pltpu.make_async_copy(grad_hbm.at[:, share_of(g)], cols.at[g, core, place], local_sem.at[0]),
        pltpu.make_async_copy(grad_hbm, full.at[core, place], local_sem.at[1]),
        pltpu.make_async_copy(hidden_hbm, hid.at[g], local_sem.at[2]),
        pltpu.make_async_copy(down_hbm, down, local_sem.at[3]),
    ]
    for copy in small + own:
        copy.start()

    barrier = pltpu.get_barrier_semaphore()

    @pl.loop(1, groups)
    def _(d):
        pl.semaphore_signal(barrier, inc=1, device_id=(me, lax.rem(g + d, groups)), device_id_type=MESH)

    @pl.loop(1, half)
    def _(d):
        pl.semaphore_signal(barrier, inc=1, device_id=(lax.rem(me + 2 * d, hosts), g), device_id_type=MESH)

    pl.semaphore_signal(barrier, inc=1, device_id=(sibling, g), device_id_type=MESH)
    for copy in small:
        copy.wait()

    row = lax.broadcasted_iota(jnp.int32, (LANES, tokens), 0)
    dense = jnp.zeros((LANES, tokens), jnp.float32)
    for k in range(ids_ref.shape[0]):
        dense = dense + jnp.where(ids_ref[k : k + 1, :] == row, weight_ref[k : k + 1, :], 0.0)
    wts[g, core, place] = dense.T

    pl.semaphore_wait(barrier, groups + half - 1)

    def z_copies(d, sender):
        q = lax.rem(g + groups - d, groups) if sender else lax.rem(g + d, groups)
        slot = q if sender else g
        return (
            remote(grad_ref.at[:, share_of(q)], cols.at[slot, core, place], zs_sem.at[d, 0], zr_sem.at[d, 0], me, q),
            remote(wts.at[g, core, place], wts.at[slot, core, place], zs_sem.at[d, 1], zr_sem.at[d, 1], me, q),
        )

    @pl.loop(1, groups)
    def _(d):
        for copy in z_copies(d, False):
            copy.start()

    def p_copy(d, kind, peer_place):
        peer = lax.rem(me + 2 * d, hosts)
        src, dst = (
            (grad_ref, full.at[core, peer_place]),
            (cols.at[:, core, peer_place], cols.at[:, core, peer_place]),
            (wts.at[:, core, peer_place], wts.at[:, core, peer_place]),
        )[kind]
        return remote(src, dst, ps_sem.at[d, kind], pr_sem.at[d, kind], peer, g)

    @pl.loop(1, half)
    def _(d):
        p_copy(d, 0, place).start()

    def h_copy(way, block, expert):
        target = g + 1 if way == 0 else g - 1
        part = hid.at[block, expert]
        return remote(part, part, hs_sem.at[way, block, expert], hr_sem.at[block, expert], me, target)

    def y_copy(block):
        return remote(hid.at[block, 1], mate.at[block], ys_sem.at[block], yr_sem.at[block], partner, g)

    own[2].wait()

    def forward(block, expert):
        @pl.when((g < groups - 1) & (block <= g))
        def _():
            h_copy(0, block, expert).start()

        @pl.when((g > 0) & (block >= g))
        def _():
            h_copy(1, block, expert).start()

    forward(g, 1)
    forward(g, 0)

    own[0].wait()
    own[1].wait()

    @pl.loop(1, groups)
    def _(d):
        for copy in z_copies(d, True):
            copy.wait_recv()

    @pl.loop(1, half)
    def _(d):
        p_copy(d, 1, place).start()
        p_copy(d, 2, place).start()

    y_copy(g).start()

    @pl.loop(1, half)
    def _(d):
        source = lax.rem(place + half - d, half)
        for kind in range(3):
            p_copy(d, kind, source).wait_recv()

    def s_copy(kind, c):
        src = (full.at[c], cols.at[:, c], wts.at[:, c])[kind]
        return remote(src, src, ss_sem.at[kind], sr_sem.at[kind], sibling, g)

    for kind in range(3):
        s_copy(kind, core).start()

    def arrive(block, expert):
        @pl.when((block >= 0) & (block < groups))
        def _():
            h_copy(0, block, expert).wait_recv()
            forward(block, expert)
            if expert == 1:
                y_copy(block).start()

    for block in (g - 1, g + 1):
        arrive(block, 1)

    for kind in range(3):
        s_copy(kind, 1 - core).wait_recv()

    lane = lax.broadcasted_iota(jnp.int32, (1, hosts), 1)
    flag = jnp.sum(jnp.where(lane == me, flags_ref[...].astype(jnp.float32), 0.0), axis=1, keepdims=True)
    shift = tokens.bit_length() - 1
    early = lax.broadcasted_iota(jnp.int32, (count, count), 0)
    late = lax.broadcasted_iota(jnp.int32, (count, count), 1)
    before = (early < late) & (lax.shift_right_logical(early, shift) == lax.shift_right_logical(late, shift))
    before = jnp.where(before, 1.0, 0.0).astype(jnp.bfloat16)
    block_of = lax.shift_right_logical(lax.broadcasted_iota(jnp.int32, (1, count), 1), shift)
    host_of = jnp.where(block_of >= half, 2 * (block_of - half) + 1, 2 * block_of)
    slot_iota = lax.broadcasted_iota(jnp.int32, (slots, count), 0)

    def selection(q, which):
        expert = 2 * (partner if which == 2 else me) + (0 if which == 0 else 1)
        weight = table[0, pl.ds(expert, 1), :]
        position = table[1, pl.ds(expert, 1), :].astype(jnp.int32)
        slot = jnp.where(weight > 0.0, host_of * capacity + position, -1)
        hit = slot_iota == slot
        pick = jnp.where(hit, 1.0, 0.0)
        held = jnp.sum(jnp.where(hit, weight, 0.0), axis=1, keepdims=True)
        return pick.astype(jnp.bfloat16), held

    def fill_table(q):
        dense = wts[q].reshape(count, LANES).T
        table[0] = dense
        chosen = jnp.where(dense > 0.0, 1.0, 0.0).astype(jnp.bfloat16)
        table[1] = dot(chosen, before, ((1,), (0,)))

    @pl.loop(0, groups)
    def _(q):
        fill_table(q)
        rows = cols[q].reshape(count, share)
        for which in range(3):
            pick, held = selection(q, which)
            scale = held if which == 0 else held * (flag if which == 2 else 1.0 - flag)
            gbuf[q, which] = (dot(pick, rows, ((1,), (0,))) * scale).astype(jnp.bfloat16)

    own[3].wait()
    fill_table(g)
    everything = full[...].reshape(count, width)
    for which in range(2):
        pick, held = selection(g, which)
        slot_rows = (dot(pick, everything, ((1,), (0,))) * held).astype(jnp.bfloat16)
        hidden_out[which] = dot(slot_rows, down[which], ((1,), (1,))).astype(hidden_out.dtype)

    for block in (g - 1, g + 1):
        arrive(block, 0)

    def first(block):
        total[0] += dot(hid[block, 0], gbuf[block, 0], ((0,), (0,)))

    def second_product(block):
        y_copy(block).wait_recv()
        return dot(hid[block, 1], gbuf[block, 1], ((0,), (0,))) + dot(mate[block], gbuf[block, 2], ((0,), (0,)))

    def second(block):
        total[1] += second_product(block)

    total[...] = jnp.zeros_like(total)
    first(g)
    second(g)

    def around(k, act):
        for block in (g - k, g + k):
            @pl.when((block >= 0) & (block < groups))
            def _():
                act(block)

    @pl.loop(2, groups)
    def _(k):
        for block in (g - k, g + k):
            arrive(block, 1)
        around(k - 1, first)

        @pl.when(k == groups - 1)
        def _():
            around(k - 1, second)

        for block in (g - k, g + k):
            arrive(block, 0)

        @pl.when(k < groups - 1)
        def _():
            around(k - 1, second)

    edge = (g == 0) | (g == groups - 1)

    @pl.when(edge)
    def _():
        block = jnp.where(g == 0, groups - 1, 0)
        down_out[0] = (total[0] + dot(hid[block, 0], gbuf[block, 0], ((0,), (0,)))).astype(down_out.dtype)
        down_out[1] = (total[1] + second_product(block)).astype(down_out.dtype)

    @pl.when(jnp.logical_not(edge))
    def _():
        down_out[...] = total[...].astype(down_out.dtype)

    @pl.loop(1, groups)
    def _(d):
        for copy in z_copies(d, False):
            copy.wait_send()

    @pl.loop(1, half)
    def _(d):
        for kind in range(3):
            p_copy(d, kind, place).wait_send()

    for kind in range(3):
        s_copy(kind, core).wait_send()

    @pl.loop(0, groups)
    def _(block):
        y_copy(block).wait_send()
        for expert in range(2):
            @pl.when((g < groups - 1) & (block <= g))
            def _():
                h_copy(0, block, expert).wait_send()

            @pl.when((g > 0) & (block >= g))
            def _():
                h_copy(1, block, expert).wait_send()


def finish(hidden_in, down_in, hidden_out, down_out, sem):
    copies = [
        pltpu.make_async_copy(hidden_in, hidden_out, sem.at[0]),
        pltpu.make_async_copy(down_in, down_out, sem.at[1]),
    ]
    for copy in copies:
        copy.start()
    for copy in copies:
        copy.wait()


def body(out_grad, expert_ids, route_weights, saved_hidden, w_down, swap_flags):
    hosts, groups = lax.axis_size("expert"), lax.axis_size("dp")
    local, slots, units = saved_hidden.shape
    tokens, width = out_grad.shape
    share = width // groups
    half = hosts // 2
    vmem = pl.BlockSpec(memory_space=pltpu.VMEM)
    hbm = pl.BlockSpec(memory_space=pl.ANY)
    dma = pltpu.SemaphoreType.DMA
    shapes = (
        jax.ShapeDtypeStruct((local, slots, units), jnp.bfloat16),
        jax.ShapeDtypeStruct((local, units, share), jnp.bfloat16),
    )
    kept = 2 * local * units * (slots + share) + SPARE
    results = pl.pallas_call(
        functools.partial(kernel, hosts, groups, slots // hosts),
        out_shape=tuple(pltpu.VMEM(x.shape, x.dtype) for x in shapes),
        in_specs=[pl.BlockSpec(memory_space=pltpu.HBM)] * 6,
        out_specs=(vmem, vmem),
        scratch_shapes=[
            pltpu.VMEM(out_grad.shape, out_grad.dtype),
            pltpu.VMEM(expert_ids.shape[::-1], expert_ids.dtype),
            pltpu.VMEM(route_weights.shape[::-1], route_weights.dtype),
            pltpu.VMEM(swap_flags.shape[::-1], swap_flags.dtype),
            pltpu.VMEM((groups, local, slots, units), jnp.bfloat16),
            pltpu.VMEM((groups, slots, units), jnp.bfloat16),
            pltpu.VMEM((groups, 2, half, tokens, LANES), jnp.float32),
            pltpu.VMEM((2, half, tokens, width), jnp.bfloat16),
            pltpu.VMEM((groups, 2, half, tokens, share), jnp.bfloat16),
            pltpu.VMEM((2, LANES, hosts * tokens), jnp.float32),
            pltpu.VMEM((groups, 3, slots, share), jnp.bfloat16),
            pltpu.VMEM((local, units, share), jnp.float32),
            pltpu.VMEM(w_down.shape, jnp.bfloat16),
            dma((8,)),
            dma((groups, 2)), dma((groups, 2)),
            dma((half, 3)), dma((half, 3)),
            dma((3,)), dma((3,)),
            dma((2, groups, 2)), dma((groups, 2)),
            dma((groups,)), dma((groups,)),
        ],
        compiler_params=pltpu.CompilerParams(
            collective_id=0, has_side_effects=True, vmem_limit_bytes=VMEM_BYTES - kept
        ),
    )(out_grad, expert_ids.T, route_weights.T, swap_flags.T, saved_hidden, w_down)
    return pl.pallas_call(
        finish,
        out_shape=shapes,
        in_specs=[vmem, vmem],
        out_specs=(hbm, hbm),
        scratch_shapes=[dma((2,))],
        compiler_params=pltpu.CompilerParams(vmem_limit_bytes=8 * 1024 * 1024),
    )(*results)


def solution(mesh):
    in_specs = (
        P(("expert", "dp"), None),
        P(("expert", "dp"), None),
        P(("expert", "dp"), None),
        P("expert", "dp", None),
        P("expert", None, None),
        P(None, "dp"),
    )
    out_specs = (P("expert", "dp", None), P("expert", None, "dp"))
    return jax.shard_map(body, mesh=mesh, in_specs=in_specs, out_specs=out_specs, check_vma=False)
```

```python
import functools

import jax
import jax.numpy as jnp
from jax import lax
from jax.experimental import pallas as pl
from jax.experimental.pallas import tpu as pltpu
from jax.sharding import PartitionSpec as P

MESH = pl.DeviceIdType.MESH
LANES = 128
VMEM_BYTES = 67_043_328
SPARE = 1024 * 1024


def dot(a, b, dims):
    return lax.dot_general(a, b, (dims, ((), ())), preferred_element_type=jnp.float32)


def kernel(
    hosts, groups, capacity,
    grad_hbm, ids_hbm, weight_hbm, flags_hbm, hidden_hbm, down_hbm,
    hidden_out, down_out,
    grad_ref, ids_ref, weight_ref, flags_ref,
    hid, mate, wts, full, cols, table, gbuf, total, down,
    local_sem,
    zs_sem, zr_sem,
    ps_sem, pr_sem,
    ss_sem, sr_sem,
    hs_sem, hr_sem,
    ys_sem, yr_sem,
):
    half = hosts // 2
    me = lax.axis_index("expert")
    g = lax.axis_index("dp")
    core, place = lax.rem(me, 2), lax.div(me, 2)
    sibling = me + 1 - 2 * core
    partner = lax.rem(me + half, hosts)
    tokens, width = grad_ref.shape
    slots, units = hidden_hbm.shape[1:]
    share = width // groups
    count = hosts * tokens

    def to(host, group):
        return {"expert": host, "dp": group}

    def remote(src, dst, send, recv, host, group):
        return pltpu.make_async_remote_copy(
            src_ref=src, dst_ref=dst, send_sem=send, recv_sem=recv,
            device_id=(host, group), device_id_type=MESH,
        )

    def share_of(group):
        return pl.ds(pl.multiple_of(group * share, LANES), share)

    small = [
        pltpu.make_async_copy(ids_hbm, ids_ref, local_sem.at[4]),
        pltpu.make_async_copy(weight_hbm, weight_ref, local_sem.at[5]),
        pltpu.make_async_copy(grad_hbm, grad_ref, local_sem.at[6]),
        pltpu.make_async_copy(flags_hbm, flags_ref, local_sem.at[7]),
    ]
    own = [
        pltpu.make_async_copy(grad_hbm.at[:, share_of(g)], cols.at[g, core, place], local_sem.at[0]),
        pltpu.make_async_copy(grad_hbm, full.at[core, place], local_sem.at[1]),
        pltpu.make_async_copy(hidden_hbm, hid.at[g], local_sem.at[2]),
        pltpu.make_async_copy(down_hbm, down, local_sem.at[3]),
    ]
    for copy in small + own:
        copy.start()

    barrier = pltpu.get_barrier_semaphore()

    @pl.loop(1, groups)
    def _(d):
        pl.semaphore_signal(barrier, inc=1, device_id=(me, lax.rem(g + d, groups)), device_id_type=MESH)

    @pl.loop(1, half)
    def _(d):
        pl.semaphore_signal(barrier, inc=1, device_id=(lax.rem(me + 2 * d, hosts), g), device_id_type=MESH)

    pl.semaphore_signal(barrier, inc=1, device_id=(sibling, g), device_id_type=MESH)
    for copy in small:
        copy.wait()

    row = lax.broadcasted_iota(jnp.int32, (LANES, tokens), 0)
    dense = jnp.zeros((LANES, tokens), jnp.float32)
    for k in range(ids_ref.shape[0]):
        dense = dense + jnp.where(ids_ref[k : k + 1, :] == row, weight_ref[k : k + 1, :], 0.0)
    wts[g, core, place] = dense.T

    pl.semaphore_wait(barrier, groups + half - 1)

    def z_copies(d, sender):
        q = lax.rem(g + groups - d, groups) if sender else lax.rem(g + d, groups)
        slot = q if sender else g
        return (
            remote(grad_ref.at[:, share_of(q)], cols.at[slot, core, place], zs_sem.at[d, 0], zr_sem.at[d, 0], me, q),
            remote(wts.at[g, core, place], wts.at[slot, core, place], zs_sem.at[d, 1], zr_sem.at[d, 1], me, q),
        )

    @pl.loop(1, groups)
    def _(d):
        for copy in z_copies(d, False):
            copy.start()

    def p_copy(d, kind, peer_place):
        peer = lax.rem(me + 2 * d, hosts)
        src, dst = (
            (grad_ref, full.at[core, peer_place]),
            (cols.at[:, core, peer_place], cols.at[:, core, peer_place]),
            (wts.at[:, core, peer_place], wts.at[:, core, peer_place]),
        )[kind]
        return remote(src, dst, ps_sem.at[d, kind], pr_sem.at[d, kind], peer, g)

    @pl.loop(1, half)
    def _(d):
        p_copy(d, 0, place).start()

    def rows_of(part):
        return pl.ds((part - 1) * (slots // 2), slots // 2)

    def piece(block, part):
        return hid.at[block, 0] if part == 0 else hid.at[block, 1, rows_of(part)]

    def h_copy(way, block, expert):
        target = g + 1 if way == 0 else g - 1
        part = piece(block, expert)
        return remote(part, part, hs_sem.at[way, block, expert], hr_sem.at[block, expert], me, target)

    def y_copy(block, part):
        return remote(
            piece(block, part), mate.at[block, rows_of(part)],
            ys_sem.at[block, part - 1], yr_sem.at[block, part - 1], partner, g,
        )

    own[2].wait()

    def forward(block, expert):
        @pl.when((g < groups - 1) & (block <= g))
        def _():
            h_copy(0, block, expert).start()

        @pl.when((g > 0) & (block >= g))
        def _():
            h_copy(1, block, expert).start()

    for part in (1, 2, 0):
        forward(g, part)

    own[0].wait()
    own[1].wait()

    @pl.loop(1, groups)
    def _(d):
        for copy in z_copies(d, True):
            copy.wait_recv()

    @pl.loop(1, half)
    def _(d):
        p_copy(d, 1, place).start()
        p_copy(d, 2, place).start()

    for part in (1, 2):
        y_copy(g, part).start()

    @pl.loop(1, half)
    def _(d):
        source = lax.rem(place + half - d, half)
        for kind in range(3):
            p_copy(d, kind, source).wait_recv()

    def s_copy(kind, c):
        src = (full.at[c], cols.at[:, c], wts.at[:, c])[kind]
        return remote(src, src, ss_sem.at[kind], sr_sem.at[kind], sibling, g)

    for kind in range(3):
        s_copy(kind, core).start()

    def arrive(block, expert):
        @pl.when((block >= 0) & (block < groups))
        def _():
            h_copy(0, block, expert).wait_recv()
            forward(block, expert)
            if expert > 0:
                y_copy(block, expert).start()

    for part in (1, 2):
        for block in (g - 1, g + 1):
            arrive(block, part)

    for kind in range(3):
        s_copy(kind, 1 - core).wait_recv()

    lane = lax.broadcasted_iota(jnp.int32, (1, hosts), 1)
    flag = jnp.sum(jnp.where(lane == me, flags_ref[...].astype(jnp.float32), 0.0), axis=1, keepdims=True)
    shift = tokens.bit_length() - 1
    early = lax.broadcasted_iota(jnp.int32, (count, count), 0)
    late = lax.broadcasted_iota(jnp.int32, (count, count), 1)
    before = (early < late) & (lax.shift_right_logical(early, shift) == lax.shift_right_logical(late, shift))
    before = jnp.where(before, 1.0, 0.0).astype(jnp.bfloat16)
    block_of = lax.shift_right_logical(lax.broadcasted_iota(jnp.int32, (1, count), 1), shift)
    host_of = jnp.where(block_of >= half, 2 * (block_of - half) + 1, 2 * block_of)
    slot_iota = lax.broadcasted_iota(jnp.int32, (slots, count), 0)

    def selection(q, which):
        expert = 2 * (partner if which == 2 else me) + (0 if which == 0 else 1)
        weight = table[0, pl.ds(expert, 1), :]
        position = table[1, pl.ds(expert, 1), :].astype(jnp.int32)
        slot = jnp.where(weight > 0.0, host_of * capacity + position, -1)
        hit = slot_iota == slot
        pick = jnp.where(hit, 1.0, 0.0)
        held = jnp.sum(jnp.where(hit, weight, 0.0), axis=1, keepdims=True)
        return pick.astype(jnp.bfloat16), held

    def fill_table(q):
        dense = wts[q].reshape(count, LANES).T
        table[0] = dense
        chosen = jnp.where(dense > 0.0, 1.0, 0.0).astype(jnp.bfloat16)
        table[1] = dot(chosen, before, ((1,), (0,)))

    @pl.loop(0, groups)
    def _(q):
        fill_table(q)
        rows = cols[q].reshape(count, share)
        for which in range(3):
            pick, held = selection(q, which)
            scale = held if which == 0 else held * (flag if which == 2 else 1.0 - flag)
            gbuf[q, which] = (dot(pick, rows, ((1,), (0,))) * scale).astype(jnp.bfloat16)

    own[3].wait()
    fill_table(g)
    everything = full[...].reshape(count, width)
    for which in range(2):
        pick, held = selection(g, which)
        slot_rows = (dot(pick, everything, ((1,), (0,))) * held).astype(jnp.bfloat16)
        hidden_out[which] = dot(slot_rows, down[which], ((1,), (1,))).astype(hidden_out.dtype)

    for block in (g - 1, g + 1):
        arrive(block, 0)

    def first(block):
        total[0] += dot(hid[block, 0], gbuf[block, 0], ((0,), (0,)))

    def second_product(block):
        for part in (1, 2):
            y_copy(block, part).wait_recv()
        return dot(hid[block, 1], gbuf[block, 1], ((0,), (0,))) + dot(mate[block], gbuf[block, 2], ((0,), (0,)))

    def second(block):
        total[1] += second_product(block)

    total[...] = jnp.zeros_like(total)
    first(g)
    second(g)

    def around(k, act):
        for block in (g - k, g + k):
            @pl.when((block >= 0) & (block < groups))
            def _():
                act(block)

    @pl.loop(2, groups)
    def _(k):
        for part in (1, 2):
            for block in (g - k, g + k):
                arrive(block, part)
        around(k - 1, first)

        @pl.when(k == groups - 1)
        def _():
            around(k - 1, second)

        for block in (g - k, g + k):
            arrive(block, 0)

        @pl.when(k < groups - 1)
        def _():
            around(k - 1, second)

    edge = (g == 0) | (g == groups - 1)

    @pl.when(edge)
    def _():
        block = jnp.where(g == 0, groups - 1, 0)
        down_out[0] = (total[0] + dot(hid[block, 0], gbuf[block, 0], ((0,), (0,)))).astype(down_out.dtype)
        down_out[1] = (total[1] + second_product(block)).astype(down_out.dtype)

    @pl.when(jnp.logical_not(edge))
    def _():
        down_out[...] = total[...].astype(down_out.dtype)

    @pl.loop(1, groups)
    def _(d):
        for copy in z_copies(d, False):
            copy.wait_send()

    @pl.loop(1, half)
    def _(d):
        for kind in range(3):
            p_copy(d, kind, place).wait_send()

    for kind in range(3):
        s_copy(kind, core).wait_send()

    @pl.loop(0, groups)
    def _(block):
        for part in (1, 2):
            y_copy(block, part).wait_send()
        for expert in range(3):
            @pl.when((g < groups - 1) & (block <= g))
            def _():
                h_copy(0, block, expert).wait_send()

            @pl.when((g > 0) & (block >= g))
            def _():
                h_copy(1, block, expert).wait_send()


def finish(hidden_in, down_in, hidden_out, down_out, sem):
    copies = [
        pltpu.make_async_copy(hidden_in, hidden_out, sem.at[0]),
        pltpu.make_async_copy(down_in, down_out, sem.at[1]),
    ]
    for copy in copies:
        copy.start()
    for copy in copies:
        copy.wait()


def body(out_grad, expert_ids, route_weights, saved_hidden, w_down, swap_flags):
    hosts, groups = lax.axis_size("expert"), lax.axis_size("dp")
    local, slots, units = saved_hidden.shape
    tokens, width = out_grad.shape
    share = width // groups
    half = hosts // 2
    vmem = pl.BlockSpec(memory_space=pltpu.VMEM)
    hbm = pl.BlockSpec(memory_space=pl.ANY)
    dma = pltpu.SemaphoreType.DMA
    shapes = (
        jax.ShapeDtypeStruct((local, slots, units), jnp.bfloat16),
        jax.ShapeDtypeStruct((local, units, share), jnp.bfloat16),
    )
    kept = 2 * local * units * (slots + share) + SPARE
    results = pl.pallas_call(
        functools.partial(kernel, hosts, groups, slots // hosts),
        out_shape=tuple(pltpu.VMEM(x.shape, x.dtype) for x in shapes),
        in_specs=[pl.BlockSpec(memory_space=pltpu.HBM)] * 6,
        out_specs=(vmem, vmem),
        scratch_shapes=[
            pltpu.VMEM(out_grad.shape, out_grad.dtype),
            pltpu.VMEM(expert_ids.shape[::-1], expert_ids.dtype),
            pltpu.VMEM(route_weights.shape[::-1], route_weights.dtype),
            pltpu.VMEM(swap_flags.shape[::-1], swap_flags.dtype),
            pltpu.VMEM((groups, local, slots, units), jnp.bfloat16),
            pltpu.VMEM((groups, slots, units), jnp.bfloat16),
            pltpu.VMEM((groups, 2, half, tokens, LANES), jnp.float32),
            pltpu.VMEM((2, half, tokens, width), jnp.bfloat16),
            pltpu.VMEM((groups, 2, half, tokens, share), jnp.bfloat16),
            pltpu.VMEM((2, LANES, hosts * tokens), jnp.float32),
            pltpu.VMEM((groups, 3, slots, share), jnp.bfloat16),
            pltpu.VMEM((local, units, share), jnp.float32),
            pltpu.VMEM(w_down.shape, jnp.bfloat16),
            dma((8,)),
            dma((groups, 2)), dma((groups, 2)),
            dma((half, 3)), dma((half, 3)),
            dma((3,)), dma((3,)),
            dma((2, groups, 3)), dma((groups, 3)),
            dma((groups, 2)), dma((groups, 2)),
        ],
        compiler_params=pltpu.CompilerParams(
            collective_id=0, has_side_effects=True, vmem_limit_bytes=VMEM_BYTES - kept
        ),
    )(out_grad, expert_ids.T, route_weights.T, swap_flags.T, saved_hidden, w_down)
    return pl.pallas_call(
        finish,
        out_shape=shapes,
        in_specs=[vmem, vmem],
        out_specs=(hbm, hbm),
        scratch_shapes=[dma((2,))],
        compiler_params=pltpu.CompilerParams(vmem_limit_bytes=8 * 1024 * 1024),
    )(*results)


def solution(mesh):
    in_specs = (
        P(("expert", "dp"), None),
        P(("expert", "dp"), None),
        P(("expert", "dp"), None),
        P("expert", "dp", None),
        P("expert", None, None),
        P(None, "dp"),
    )
    out_specs = (P("expert", "dp", None), P("expert", None, "dp"))
    return jax.shard_map(body, mesh=mesh, in_specs=in_specs, out_specs=out_specs, check_vma=False)
```
